32 devices in a mesh: integral: 4 (over x, core), pair: 8 (over z, y).
Axes of the slice: x: 2, y: 2, z: 4, core: 2. Of those that a mesh axis runs over, the one named last changes fastest.
Arguments:
- t2_tiles: bfloat16 [1024, 20, 1024], P('pair', None, 'integral'), may hold values from -6 to 6
- keep_tile: int32 [20], replicated, may hold values from 0 to 31, as said below
- integrals: bfloat16 [32, 1024, 4096], P('pair', None, 'integral'), may hold values from -0.078125 to 0.078125
Outputs:
- residual: bfloat16 [1024, 4096], P('pair', 'integral')
The draws below stay inside these ranges and needn't reach their ends.
Inputs may be any that keep to these rules, and one draw needn't show every extreme that they name: `keep_tile`: 20 distinct tile numbers in no particular order; tile k lies in the integral rows of pair index k // 4; at least one pair index has all 4 of its tiles listed.
All inputs are finite; a program needn't handle non-finite values.
Results may differ from the reference program's by a relative error of at most 0.0014.
Values may be sent and summed in bfloat16 or wider, within the bound.
A program may use at most 128 MiB of HBM per device.

```python
import jax
import jax.numpy as jnp
from jax import lax

TT = 1024
KT_DEV = 4
KT = 32
NKEEP = 20
OPAIRS = 1024
QW = 4096


def draw_keep_tile(key, part):
    owner_total = KT // KT_DEV
    first_key, second_key, third_key = jax.random.split(key, 3)
    full_owner = jax.random.randint(first_key, (), 0, owner_total)
    tile_ids = jnp.arange(KT, dtype=jnp.int32)
    shuffled = jax.random.permutation(second_key, KT).astype(jnp.int32)
    scores = jnp.where(tile_ids // KT_DEV == full_owner, tile_ids - KT, shuffled)
    picked = jnp.argsort(scores, stable=True)[:NKEEP]
    return picked[jax.random.permutation(third_key, NKEEP)].astype(jnp.int32)


def level_of(stream_key, extent, pieces, low, largest):
    factor_of = 1.0
    for position, blocks in pieces:
        heights = jax.random.uniform(jax.random.fold_in(jax.random.fold_in(stream_key, 6), position), (blocks,), jnp.float32, low / len(pieces), largest / len(pieces))
        factor_of = factor_of * jnp.repeat(jnp.exp(heights), extent[position] // blocks).reshape((-1,) + (1,) * (len(extent) - 1 - position))
    return factor_of


def gaussian(own_key, shape, spread, most, cuts=(), held_as=jnp.bfloat16):
    entries = jax.random.normal(own_key, shape, jnp.float32) * spread
    if len(cuts) > 0:
        entries = level_of(own_key, shape, cuts, -0.22, 0.18) * entries
    return jnp.clip(entries, min=-most, max=most).astype(held_as)


def setup_inputs(seed: int = 0) -> dict:
    seeds = jax.random.split(jax.random.key(seed), 4)
    t2_tiles = gaussian(seeds[0], (OPAIRS, NKEEP, TT), 1.0, 6.0, ((0, 8), (2, 4)))
    keep_tile = draw_keep_tile(jax.random.fold_in(seeds[3], 71), 0)
    integrals = gaussian(seeds[2], (KT, TT, QW), (NKEEP * TT // 4) ** -0.5, 0.078125, ((0, 8), (2, 4)))
    return {"t2_tiles": t2_tiles, "keep_tile": keep_tile, "integrals": integrals}


def reference(t2_tiles, keep_tile, integrals):
    def add_tile(running, inputs):
        amp_rows, tile_number = inputs
        v_rows = lax.dynamic_index_in_dim(integrals, tile_number, 0, keepdims=False)
        return running + jnp.dot(amp_rows, v_rows, preferred_element_type=jnp.float32), None

    start_sum = jnp.zeros((t2_tiles.shape[0], integrals.shape[2]), jnp.float32)
    partial_value, _ = lax.scan(add_tile, start_sum, (jnp.swapaxes(t2_tiles, 0, 1), keep_tile.astype(jnp.int32)))
    return (0.5 * partial_value).astype(jnp.bfloat16)
```

```python
import functools
import itertools

import jax
import jax.numpy as jnp
from jax import lax
from jax.experimental import pallas as pl
from jax.experimental.pallas import tpu as pltpu
from jax.sharding import PartitionSpec as P

MESH = pl.DeviceIdType.MESH
CORES = 2
HALVES = 2
CUTS = 2
AHEAD = ((-1, -1), (-1, -1), (-1, 1), (3, 4))
LAG = 2
LANES = 128
SUB = 8
LEVELS = 32766.0
TINY = 2e-34


def inner_of(count):
    return 2 ** ((count.bit_length() - 1) // 2)


def plan_of(count, cuts):
    steps = count * cuts
    if count & (count - 1):
        order = [[(k - z) % count for k in range(2 * z, 2 * z + count)] for z in range(count)]
    else:
        order = [[z ^ k ^ (k >> 1) for k in range(count)] for z in range(count)]
    late = {}
    for zc in range(count):
        for zs in (range(zc), range(count - 1, zc, -1)):
            before = None
            for z in zs:
                for r in range(cuts):
                    ready = order[z].index(zc) * cuts + r + 2
                    late[z, zc, r] = ready if before is None else max(ready, late[before, zc, r] + LAG)
                before = z
    last = max(late.values())
    passes = [[[[] for _ in range(count)] for _ in range(cuts)] for _ in range(last + 1)]
    for (z, zc, r), at in late.items():
        if 0 < z < count - 1:
            passes[at][r][z].append(zc)
    return order, passes, max(last + 1, steps + 2)


def release(k, r):
    return AHEAD[k][r] if k < len(AHEAD) else AHEAD[-1][r] + (k + 1 - len(AHEAD)) * CUTS


def ladder_kernel(
    dims, keep_ref, t2_ref, v_ref, out_ref,
    tiles, packed, amps, ints, part, y_out, y_scale, y_in, y_in_scale, z_out, z_scale, z_in, z_in_scale,
    v_sem, t_sem, own_sem, a_send, a_recv, x_send, x_recv, c_send, c_recv, y_send, y_recv, z_send, z_recv,
):
    np_, ny, ni, slots, rows, cols = dims
    nz, nx = np_ // ny, ni // CORES
    piece = rows // CUTS
    kept = t2_ref.shape[0]
    qw = v_ref.shape[2]
    width = qw // HALVES
    p, i = lax.axis_index("pair"), lax.axis_index("integral")
    z, y = p // ny, p % ny
    x, c = i // CORES, i % CORES
    other = x * CORES + (1 - c)
    tables, passes, loops = plan_of(nz, CUTS)

    def pick(values):
        return sum(jnp.where(z == at, values[at], 0) for at in range(nz))

    order = [pick([tables[at][k] for at in range(nz)]) for k in range(nz)]

    load_t = pltpu.make_async_copy(t2_ref, tiles, t_sem)
    load_t.start()
    load_v = pltpu.make_async_copy(v_ref, ints, v_sem)

    barrier = pltpu.get_barrier_semaphore()
    for d in range(1, np_):
        pl.semaphore_signal(barrier, inc=1, device_id={"pair": (p + d) % np_}, device_id_type=MESH)
    for d in range(1, nx):
        pl.semaphore_signal(
            barrier, inc=1, device_id={"integral": ((x + d) % nx) * CORES + c}, device_id_type=MESH
        )
    pl.semaphore_signal(barrier, inc=1, device_id={"integral": other}, device_id_type=MESH)

    def places(owner):
        found = []
        for s in range(slots):
            tile = owner * slots + s
            at = jnp.int32(kept)
            for j in range(kept):
                at = jnp.where(keep_ref[j] == tile, j, at)
            found.append(at)
        return found

    def pack(owner, r, found):
        for s in range(slots):
            tile = tiles[jnp.minimum(found[s], kept - 1), r * piece : (r + 1) * piece, :]
            packed[owner, r, s] = jnp.where(found[s] < kept, tile, jnp.zeros_like(tile))

    def block(source, r, part_i):
        start = (((source // ny) * CUTS + r) * ny + source % ny) * piece
        return amps.at[:, pl.ds(pl.multiple_of(start, piece), piece), pl.ds(pl.multiple_of(part_i * cols, cols), cols)]

    def a_copy(dest, source, r):
        return pltpu.make_async_remote_copy(
            src_ref=packed.at[dest, r], dst_ref=block(source, r, i),
            send_sem=a_send.at[dest, r], recv_sem=a_recv.at[source, r],
            device_id={"pair": dest}, device_id_type=MESH,
        )

    def x_copy(source, r, dest_x, from_x):
        region = block(source, r, from_x * CORES + c)
        return pltpu.make_async_remote_copy(
            src_ref=region, dst_ref=region, send_sem=x_send.at[dest_x, source, r], recv_sem=x_recv.at[from_x, source, r],
            device_id={"integral": dest_x * CORES + c}, device_id_type=MESH,
        )

    def c_copy(source, r, part_x, part_c):
        region = block(source, r, part_x * CORES + part_c)
        return pltpu.make_async_remote_copy(
            src_ref=region, dst_ref=region, send_sem=c_send.at[part_x, source, r], recv_sem=c_recv.at[part_x, source, r],
            device_id={"integral": other}, device_id_type=MESH,
        )

    def own_copy(r):
        return pltpu.make_async_copy(packed.at[p, r], block(p, r, i), own_sem.at[r])

    def y_copies(zc, r, d, h):
        pairs = ((y_out, y_in), (y_scale, y_in_scale))
        return [
            pltpu.make_async_remote_copy(
                src_ref=src.at[d - 1, zc, r, h], dst_ref=dst.at[d - 1, zc, r, h],
                send_sem=y_send.at[n, d - 1, zc, r, h], recv_sem=y_recv.at[n, d - 1, zc, r, h],
                device_id={"pair": z * ny + (y + d) % ny}, device_id_type=MESH,
            )
            for n, (src, dst) in enumerate(pairs)
        ]

    def z_copies(zc, slot, r, h):
        to = jnp.where(zc > z, p + ny, p + np_ - ny) % np_
        pairs = ((z_out, z_in), (z_scale, z_in_scale))
        return [
            pltpu.make_async_remote_copy(
                src_ref=src.at[zc, r, h], dst_ref=dst.at[slot, r, h],
                send_sem=z_send.at[n, zc, r, h], recv_sem=z_recv.at[n, slot, r, h],
                device_id={"pair": to}, device_id_type=MESH,
            )
            for n, (src, dst) in enumerate(pairs)
        ]

    def z_slot(zc):
        return jnp.where(zc == z - 1, nz, zc)

    def lanes_of(g):
        return pl.ds(pl.multiple_of(g * LANES, LANES), LANES)

    def absorb(total, code, scale):
        step = scale[...]

        @pl.loop(0, width // LANES)
        def _(g):
            at = lanes_of(g)
            gain = code[:, at].astype(jnp.float32).reshape(piece // SUB, SUB, LANES) * step[None]
            total[:, at] += gain.reshape(piece, LANES)

    def encode(total, code, scale):
        def most(g, top):
            values = jnp.abs(total[:, lanes_of(g)]).reshape(piece // SUB, SUB, LANES)
            return jnp.maximum(top, jnp.max(values, axis=0))

        top = lax.fori_loop(0, width // LANES, most, jnp.full((SUB, LANES), TINY, jnp.float32))
        scale[...] = top * (1.0 / LEVELS)
        gain = LEVELS / top

        @pl.loop(0, width // LANES)
        def _(g):
            at = lanes_of(g)
            values = total[:, at].reshape(piece // SUB, SUB, LANES) * gain[None]
            code[:, at] = jnp.round(values).reshape(piece, LANES).astype(jnp.int32).astype(jnp.int16)

    load_t.wait()
    load_v.start()
    own_places = places(p)
    for r in range(CUTS):
        pack(p, r, own_places)
        own_copy(r).start()
    pl.semaphore_wait(barrier, np_ - 1 + nx - 1 + 1)

    def send_rows(k, r):
        plane = order[k]
        for dy in range(ny):
            dest = plane * ny + (y + dy) % ny
            if k or dy:
                if r == 0:
                    found[k, dy] = places(dest)
                    for each in range(CUTS):
                        pack(dest, each, found[k, dy])
                a_copy(dest, p, r).start()

    found = {}

    def sources(k):
        zc = order[k]
        for dy in range(ny):
            yield dy, zc * ny + (y + ny - dy) % ny

    def spread_one(source, r):
        for d in range(1, nx):
            x_copy(source, r, (x + d) % nx, x).start()
        c_copy(source, r, x, c).start()

    def spread(k, r):
        for dy, source in sources(k):
            if k or dy:
                a_copy(p, source, r).wait_recv()
                spread_one(source, r)

    def first():
        for r in range(CUTS):
            own_copy(r).wait()
            spread_one(p, r)
            for k in range(nz):
                if release(k, r) < 0:
                    send_rows(k, r)

    def forward(k, r):
        for dy, source in sources(k):
            for d in range(1, nx):
                from_x = (x + d) % nx
                x_copy(source, r, x, from_x).wait_recv()
                c_copy(source, r, from_x, c).start()

    def multiply(k, r):
        zc = order[k]
        for dy, source in sources(k):
            for xx in range(nx):
                c_copy(source, r, xx, 1 - c).wait_recv()
        if k == 0 and r == 0:
            load_v.wait()
        span = ny * piece
        left = pl.ds(pl.multiple_of((zc * CUTS + r) * span, span), span)
        wide = min(512, width)
        for h in range(HALVES):
            @pl.loop(0, width // wide)
            def _(n):
                right = pl.ds(pl.multiple_of(h * width + n * wide, wide), wide)
                into = pl.ds(pl.multiple_of(n * wide, wide), wide)
                total = jnp.zeros((span, wide), jnp.float32)
                for s in range(slots):
                    total += jnp.dot(amps[s, left, :], ints[s, :, right], preferred_element_type=jnp.float32)
                part[zc, r, h, :, :, into] = total.reshape(ny, piece, wide)

            for d in range(1, ny):
                encode(part.at[zc, r, h, (y + d) % ny], y_out.at[d - 1, zc, r, h], y_scale.at[d - 1, zc, r, h])
                for copy in y_copies(zc, r, d, h):
                    copy.start()

    def hand_on(zc, r, h):
        encode(part.at[zc, r, h, y], z_out.at[zc, r, h], z_scale.at[zc, r, h])
        for copy in z_copies(zc, z_slot(zc), r, h):
            copy.start()

    def take(slot, zc, r, h):
        for copy in z_copies(zc, slot, r, h):
            copy.wait_recv()
        absorb(part.at[zc, r, h, y], z_in.at[slot, r, h], z_in_scale.at[slot, r, h])

    def reduce_y(k, r):
        zc = order[k]
        for h in range(HALVES):
            for d in range(1, ny):
                for copy in y_copies(zc, r, d, h):
                    copy.wait_recv()
                absorb(part.at[zc, r, h, y], y_in.at[d - 1, zc, r, h], y_in_scale.at[d - 1, zc, r, h])
            if k > 0:
                @pl.when((z == 0) | (z == nz - 1))
                def _():
                    hand_on(zc, r, h)

    def pass_on(at):
        for r in range(CUTS):
            now = passes[at][r]
            for n in range(max(len(some) for some in now)):
                to = [some[n] if n < len(some) else -1 for some in now]
                zc = pick([max(each, 0) for each in to])

                @pl.when(pick([int(each >= 0) for each in to]) > 0)
                def _():
                    for h in range(HALVES):
                        take(zc, zc, r, h)
                        hand_on(zc, r, h)

    steps = list(itertools.product(range(nz), range(CUTS)))
    first()
    for t in range(loops):
        if t < len(steps):
            k, r = steps[t]
            for ahead in steps:
                if release(*ahead) == t:
                    send_rows(*ahead)
            spread(k, r)
        if 0 <= t - 1 < len(steps):
            forward(*steps[t - 1])
            multiply(*steps[t - 1])
        if 0 <= t - 2 < len(steps):
            reduce_y(*steps[t - 2])
        if t < len(passes):
            pass_on(t)

    for r, h in itertools.product(range(CUTS), range(HALVES)):
        @pl.when(z > 0)
        def _():
            take(z, z, r, h)

        @pl.when(z < nz - 1)
        def _():
            take(nz, z, r, h)

        out_ref[r * piece : (r + 1) * piece, h * width : (h + 1) * width] = (0.5 * part[z, r, h, y]).astype(out_ref.dtype)

    for k, r, dy in itertools.product(range(nz), range(CUTS), range(ny)):
        if k or dy:
            a_copy(order[k] * ny + (y + dy) % ny, p, r).wait_send()
    for k, r in steps:
        zc = order[k]
        for dy, source in sources(k):
            for d in range(1, nx):
                x_copy(source, r, (x + d) % nx, x).wait_send()
            for xx in range(nx):
                c_copy(source, r, xx, c).wait_send()
        for h in range(HALVES):
            for d in range(1, ny):
                for copy in y_copies(zc, r, d, h):
                    copy.wait_send()
            if k > 0:
                for copy in z_copies(zc, z_slot(zc), r, h):
                    copy.wait_send()


def on_device(t2_tiles, keep_tile, integrals):
    np_, ni = lax.axis_size("pair"), lax.axis_size("integral")
    rows, kept, cols = t2_tiles.shape
    slots, tt, qw = integrals.shape
    ny = inner_of(np_)
    nz, nx = np_ // ny, ni // CORES
    by_tile = jnp.swapaxes(t2_tiles, 0, 1)
    dma = pltpu.SemaphoreType.DMA
    piece, width = rows // CUTS, qw // HALVES
    dims = (np_, ny, ni, slots, rows, cols)
    y_lead, z_lead, in_lead = (ny - 1, nz, CUTS, HALVES), (nz, CUTS, HALVES), (nz + 1, CUTS, HALVES)
    return pl.pallas_call(
        functools.partial(ladder_kernel, dims),
        out_shape=jax.ShapeDtypeStruct((rows, qw), jnp.bfloat16),
        in_specs=[
            pl.BlockSpec(memory_space=pltpu.SMEM),
            pl.BlockSpec(memory_space=pl.ANY),
            pl.BlockSpec(memory_space=pl.ANY),
        ],
        out_specs=pl.BlockSpec(memory_space=pltpu.VMEM),
        scratch_shapes=[
            pltpu.VMEM((kept, rows, cols), jnp.bfloat16),
            pltpu.VMEM((np_, CUTS, slots, piece, cols), jnp.bfloat16),
            pltpu.VMEM((slots, np_ * rows, tt), jnp.bfloat16),
            pltpu.VMEM((slots, tt, qw), jnp.bfloat16),
            pltpu.VMEM((nz, CUTS, HALVES, ny, piece, width), jnp.float32),
            pltpu.VMEM((*y_lead, piece, width), jnp.int16),
            pltpu.VMEM((*y_lead, SUB, LANES), jnp.float32),
            pltpu.VMEM((*y_lead, piece, width), jnp.int16),
            pltpu.VMEM((*y_lead, SUB, LANES), jnp.float32),
            pltpu.VMEM((*z_lead, piece, width), jnp.int16),
            pltpu.VMEM((*z_lead, SUB, LANES), jnp.float32),
            pltpu.VMEM((*in_lead, piece, width), jnp.int16),
            pltpu.VMEM((*in_lead, SUB, LANES), jnp.float32),
            dma, dma, dma((CUTS,)),
            dma((np_, CUTS)), dma((np_, CUTS)),
            dma((nx, np_, CUTS)), dma((nx, np_, CUTS)),
            dma((nx, np_, CUTS)), dma((nx, np_, CUTS)),
            dma((2, *y_lead)), dma((2, *y_lead)),
            dma((2, *z_lead)), dma((2, *in_lead)),
        ],
        compiler_params=pltpu.CompilerParams(
            collective_id=0, has_side_effects=True, vmem_limit_bytes=60 * 1024 * 1024
        ),
    )(keep_tile.astype(jnp.int32), by_tile, integrals)


def solution(mesh):
    placed = (P("pair", None, "integral"), P(), P("pair", None, "integral"))
    return jax.shard_map(
        on_device, mesh=mesh, in_specs=placed, out_specs=P("pair", "integral"), check_vma=False
    )
```

```python
import functools
import itertools

import jax
import jax.numpy as jnp
from jax import lax
from jax.experimental import pallas as pl
from jax.experimental.pallas import tpu as pltpu
from jax.sharding import PartitionSpec as P

MESH = pl.DeviceIdType.MESH
CORES = 2
HALVES = 2
CUTS = 2
UNROLL = 4
MUL_LAG = 2
SUM_LAG = 3
WIDE = 512
AHEAD = ((-1, -1), (-1, -1), (-1, 1), (3, 4))
LAG = 2
LANES = 128
SUB = 8
LEVELS = 32766.0
TINY = 2e-34


def inner_of(count):
    return 2 ** ((count.bit_length() - 1) // 2)


def plan_of(count, cuts):
    steps = count * cuts
    if count & (count - 1):
        order = [[(k - z) % count for k in range(2 * z, 2 * z + count)] for z in range(count)]
    else:
        order = [[z ^ k ^ (k >> 1) for k in range(count)] for z in range(count)]
    late = {}
    for zc in range(count):
        for zs in (range(zc), range(count - 1, zc, -1)):
            before = None
            for z in zs:
                for r in range(cuts):
                    ready = order[z].index(zc) * cuts + r + SUM_LAG
                    late[z, zc, r] = ready if before is None else max(ready, late[before, zc, r] + LAG)
                before = z
    last = max(late.values())
    passes = [[[[] for _ in range(count)] for _ in range(cuts)] for _ in range(last + 1)]
    for (z, zc, r), at in late.items():
        if 0 < z < count - 1:
            passes[at][r][z].append(zc)
    return order, passes, max(last + 1, steps + SUM_LAG)


def release(k, r):
    return AHEAD[k][r] if k < len(AHEAD) else AHEAD[-1][r] + (k + 1 - len(AHEAD)) * CUTS


def ladder_kernel(
    dims, keep_ref, t2_ref, v_ref, out_ref,
    tiles, packed, result, amps, ints, part, y_out, y_scale, y_in, y_in_scale, z_out, z_scale, z_in, z_in_scale,
    v_sem, t_sem, own_sem, out_sem, a_send, a_recv, x_send, x_recv, c_send, c_recv, y_send, y_recv, z_send, z_recv,
):
    np_, ny, ni, slots, rows, cols = dims
    nz, nx = np_ // ny, ni // CORES
    piece = rows // CUTS
    kept = t2_ref.shape[0]
    qw = v_ref.shape[2]
    width = qw // HALVES
    p, i = lax.axis_index("pair"), lax.axis_index("integral")
    z, y = p // ny, p % ny
    x, c = i // CORES, i % CORES
    other = x * CORES + (1 - c)
    tables, passes, loops = plan_of(nz, CUTS)

    def pick(values):
        return sum(jnp.where(z == at, values[at], 0) for at in range(nz))

    order = [pick([tables[at][k] for at in range(nz)]) for k in range(nz)]

    load_t = pltpu.make_async_copy(t2_ref, tiles, t_sem)
    load_t.start()
    load_v = pltpu.make_async_copy(v_ref, ints, v_sem)

    barrier = pltpu.get_barrier_semaphore()
    for d in range(1, np_):
        pl.semaphore_signal(barrier, inc=1, device_id={"pair": (p + d) % np_}, device_id_type=MESH)
    for d in range(1, nx):
        pl.semaphore_signal(
            barrier, inc=1, device_id={"integral": ((x + d) % nx) * CORES + c}, device_id_type=MESH
        )
    pl.semaphore_signal(barrier, inc=1, device_id={"integral": other}, device_id_type=MESH)

    def places(owner):
        found = []
        for s in range(slots):
            tile = owner * slots + s
            at = jnp.int32(kept)
            for j in range(kept):
                at = jnp.where(keep_ref[j] == tile, j, at)
            found.append(at)
        return found

    def pack(owner, r, found):
        for s in range(slots):
            tile = tiles[jnp.minimum(found[s], kept - 1), r * piece : (r + 1) * piece, :]
            packed[owner, r, s] = jnp.where(found[s] < kept, tile, jnp.zeros_like(tile))

    def block(source, r, part_i):
        start = (((source // ny) * CUTS + r) * ny + source % ny) * piece
        return amps.at[part_i, :, pl.ds(pl.multiple_of(start, piece), piece), :]

    def a_copy(dest, source, r):
        return pltpu.make_async_remote_copy(
            src_ref=packed.at[dest, r], dst_ref=block(source, r, i),
            send_sem=a_send, recv_sem=a_recv.at[source, r],
            device_id={"pair": dest}, device_id_type=MESH,
        )

    def x_copy(source, r, dest_x, from_x):
        region = block(source, r, from_x * CORES + c)
        return pltpu.make_async_remote_copy(
            src_ref=region, dst_ref=region, send_sem=x_send, recv_sem=x_recv.at[from_x, source, r],
            device_id={"integral": dest_x * CORES + c}, device_id_type=MESH,
        )

    def c_copy(source, r, part_x, part_c):
        region = block(source, r, part_x * CORES + part_c)
        return pltpu.make_async_remote_copy(
            src_ref=region, dst_ref=region, send_sem=c_send, recv_sem=c_recv.at[part_x, source, r],
            device_id={"integral": other}, device_id_type=MESH,
        )

    def own_copy(r):
        return pltpu.make_async_copy(packed.at[p, r], block(p, r, i), own_sem.at[r])

    def y_copies(zc, r, d, h):
        pairs = ((y_out, y_in), (y_scale, y_in_scale))
        return [
            pltpu.make_async_remote_copy(
                src_ref=src.at[d - 1, zc, r, h], dst_ref=dst.at[d - 1, zc, r, h],
                send_sem=y_send.at[n], recv_sem=y_recv.at[n, d - 1, zc, r, h],
                device_id={"pair": z * ny + (y + d) % ny}, device_id_type=MESH,
            )
            for n, (src, dst) in enumerate(pairs)
        ]

    def z_copies(zc, slot, r, h):
        to = jnp.where(zc > z, p + ny, p + np_ - ny) % np_
        pairs = ((z_out, z_in), (z_scale, z_in_scale))
        return [
            pltpu.make_async_remote_copy(
                src_ref=src.at[zc, r, h], dst_ref=dst.at[slot, r, h],
                send_sem=z_send.at[n], recv_sem=z_recv.at[n, slot, r, h],
                device_id={"pair": to}, device_id_type=MESH,
            )
            for n, (src, dst) in enumerate(pairs)
        ]

    def z_slot(zc):
        return jnp.where(zc == z - 1, nz, zc)

    def lanes_of(g):
        return pl.ds(pl.multiple_of(g * LANES, LANES), LANES)

    def absorb(total, code, scale):
        step = scale[...]

        @pl.loop(0, width // LANES, unroll=UNROLL)
        def _(g):
            at = lanes_of(g)
            gain = code[:, at].astype(jnp.float32).reshape(piece // SUB, SUB, LANES) * step[None]
            total[:, at] += gain.reshape(piece, LANES)

    def encode(total, code, scale):
        def most(g, top):
            values = jnp.abs(total[:, lanes_of(g)]).reshape(piece // SUB, SUB, LANES)
            return jnp.maximum(top, jnp.max(values, axis=0))

        top = lax.fori_loop(0, width // LANES, most, jnp.full((SUB, LANES), TINY, jnp.float32), unroll=UNROLL)
        scale[...] = top * (1.0 / LEVELS)
        gain = LEVELS / top

        @pl.loop(0, width // LANES, unroll=UNROLL)
        def _(g):
            at = lanes_of(g)
            values = total[:, at].reshape(piece // SUB, SUB, LANES) * gain[None]
            code[:, at] = jnp.round(values).reshape(piece, LANES).astype(jnp.int32).astype(jnp.int16)

    load_t.wait()
    load_v.start()
    own_places = places(p)
    for r in range(CUTS):
        pack(p, r, own_places)
        own_copy(r).start()
    pl.semaphore_wait(barrier, np_ - 1 + nx - 1 + 1)

    def send_rows(k, r):
        plane = order[k]
        for dy in range(ny):
            dest = plane * ny + (y + dy) % ny
            if k or dy:
                if r == 0:
                    found[k, dy] = places(dest)
                    for each in range(CUTS):
                        pack(dest, each, found[k, dy])
                a_copy(dest, p, r).start()

    found = {}

    def sources(k):
        zc = order[k]
        for dy in range(ny):
            yield dy, zc * ny + (y + ny - dy) % ny

    def spread_one(source, r):
        for d in range(1, nx):
            x_copy(source, r, (x + d) % nx, x).start()
        c_copy(source, r, x, c).start()

    def spread(k, r):
        for dy, source in sources(k):
            if k or dy:
                a_copy(p, source, r).wait_recv()
                spread_one(source, r)

    def first():
        for r in range(CUTS):
            own_copy(r).wait()
            spread_one(p, r)
            for k in range(nz):
                if release(k, r) < 0:
                    send_rows(k, r)

    def forward(k, r):
        for dy, source in sources(k):
            for d in range(1, nx):
                from_x = (x + d) % nx
                x_copy(source, r, x, from_x).wait_recv()
                c_copy(source, r, from_x, c).start()

    def multiply(k, r):
        zc = order[k]
        for dy, source in sources(k):
            for xx in range(nx):
                c_copy(source, r, xx, 1 - c).wait_recv()
        if k == 0 and r == 0:
            load_v.wait()
        span = ny * piece
        left = pl.ds(pl.multiple_of((zc * CUTS + r) * span, span), span)
        wide = min(WIDE, width)
        for h in range(HALVES):
            @pl.loop(0, width // wide)
            def _(n):
                right = pl.ds(pl.multiple_of(h * width + n * wide, wide), wide)
                into = pl.ds(pl.multiple_of(n * wide, wide), wide)
                total = jnp.zeros((span, wide), jnp.float32)
                for s, at in itertools.product(range(slots), range(ni)):
                    inner = slice(at * cols, (at + 1) * cols)
                    total += jnp.dot(amps[at, s, left, :], ints[s, inner, right], preferred_element_type=jnp.float32)
                part[zc, r, h, :, :, into] = total.reshape(ny, piece, wide)

            for d in range(1, ny):
                encode(part.at[zc, r, h, (y + d) % ny], y_out.at[d - 1, zc, r, h], y_scale.at[d - 1, zc, r, h])
                for copy in y_copies(zc, r, d, h):
                    copy.start()

    def hand_on(zc, r, h):
        encode(part.at[zc, r, h, y], z_out.at[zc, r, h], z_scale.at[zc, r, h])
        for copy in z_copies(zc, z_slot(zc), r, h):
            copy.start()

    def take(slot, zc, r, h):
        for copy in z_copies(zc, slot, r, h):
            copy.wait_recv()
        absorb(part.at[zc, r, h, y], z_in.at[slot, r, h], z_in_scale.at[slot, r, h])

    def reduce_y(k, r):
        zc = order[k]
        for h in range(HALVES):
            for d in range(1, ny):
                for copy in y_copies(zc, r, d, h):
                    copy.wait_recv()
                absorb(part.at[zc, r, h, y], y_in.at[d - 1, zc, r, h], y_in_scale.at[d - 1, zc, r, h])
            if k > 0:
                @pl.when((z == 0) | (z == nz - 1))
                def _():
                    hand_on(zc, r, h)

    def pass_on(at):
        for r in range(CUTS):
            now = passes[at][r]
            for n in range(max(len(some) for some in now)):
                to = [some[n] if n < len(some) else -1 for some in now]
                zc = pick([max(each, 0) for each in to])

                @pl.when(pick([int(each >= 0) for each in to]) > 0)
                def _():
                    for h in range(HALVES):
                        take(zc, zc, r, h)
                        hand_on(zc, r, h)

    steps = list(itertools.product(range(nz), range(CUTS)))
    first()
    for t in range(loops):
        if t < len(steps):
            k, r = steps[t]
            for ahead in steps:
                if release(*ahead) == t:
                    send_rows(*ahead)
            spread(k, r)
        if 0 <= t - 1 < len(steps):
            forward(*steps[t - 1])
        if 0 <= t - MUL_LAG < len(steps):
            multiply(*steps[t - MUL_LAG])
        if 0 <= t - SUM_LAG < len(steps):
            reduce_y(*steps[t - SUM_LAG])
        if t < len(passes):
            pass_on(t)

    def sent(ref, sem):
        pltpu.make_async_copy(ref, ref, sem).wait()

    sent(packed.at[: np_ - 1], a_send)
    sent(amps.at[: nx - 1], x_send)
    sent(amps.at[:nx], c_send)
    sent(y_out, y_send.at[0])
    sent(y_scale, y_send.at[1])

    def out_copy(r):
        at = slice(r * piece, (r + 1) * piece)
        return pltpu.make_async_copy(result.at[at, :], out_ref.at[at, :], out_sem.at[r])

    for r, h in itertools.product(range(CUTS), range(HALVES)):
        @pl.when(z > 0)
        def _():
            take(z, z, r, h)

        @pl.when(z < nz - 1)
        def _():
            take(nz, z, r, h)

        result[r * piece : (r + 1) * piece, h * width : (h + 1) * width] = (0.5 * part[z, r, h, y]).astype(result.dtype)
        if h == HALVES - 1:
            out_copy(r).start()

    sent(z_out.at[: nz - 1], z_send.at[0])
    sent(z_scale.at[: nz - 1], z_send.at[1])
    for r in range(CUTS):
        out_copy(r).wait()


def on_device(t2_tiles, keep_tile, integrals):
    np_, ni = lax.axis_size("pair"), lax.axis_size("integral")
    rows, kept, cols = t2_tiles.shape
    slots, tt, qw = integrals.shape
    ny = inner_of(np_)
    nz, nx = np_ // ny, ni // CORES
    by_tile = jnp.swapaxes(t2_tiles, 0, 1)
    dma = pltpu.SemaphoreType.DMA
    piece, width = rows // CUTS, qw // HALVES
    dims = (np_, ny, ni, slots, rows, cols)
    y_lead, z_lead, in_lead = (ny - 1, nz, CUTS, HALVES), (nz, CUTS, HALVES), (nz + 1, CUTS, HALVES)
    return pl.pallas_call(
        functools.partial(ladder_kernel, dims),
        out_shape=jax.ShapeDtypeStruct((rows, qw), jnp.bfloat16),
        in_specs=[
            pl.BlockSpec(memory_space=pltpu.SMEM),
            pl.BlockSpec(memory_space=pl.ANY),
            pl.BlockSpec(memory_space=pl.ANY),
        ],
        out_specs=pl.BlockSpec(memory_space=pl.ANY),
        scratch_shapes=[
            pltpu.VMEM((kept, rows, cols), jnp.bfloat16),
            pltpu.VMEM((np_, CUTS, slots, piece, cols), jnp.bfloat16),
            pltpu.VMEM((rows, qw), jnp.bfloat16),
            pltpu.VMEM((ni, slots, np_ * rows, cols), jnp.bfloat16),
            pltpu.VMEM((slots, tt, qw), jnp.bfloat16),
            pltpu.VMEM((nz, CUTS, HALVES, ny, piece, width), jnp.float32),
            pltpu.VMEM((*y_lead, piece, width), jnp.int16),
            pltpu.VMEM((*y_lead, SUB, LANES), jnp.float32),
            pltpu.VMEM((*y_lead, piece, width), jnp.int16),
            pltpu.VMEM((*y_lead, SUB, LANES), jnp.float32),
            pltpu.VMEM((*z_lead, piece, width), jnp.int16),
            pltpu.VMEM((*z_lead, SUB, LANES), jnp.float32),
            pltpu.VMEM((*in_lead, piece, width), jnp.int16),
            pltpu.VMEM((*in_lead, SUB, LANES), jnp.float32),
            dma, dma, dma((CUTS,)), dma((CUTS,)),
            dma, dma((np_, CUTS)),
            dma, dma((nx, np_, CUTS)),
            dma, dma((nx, np_, CUTS)),
            dma((2,)), dma((2, *y_lead)),
            dma((2,)), dma((2, *in_lead)),
        ],
        compiler_params=pltpu.CompilerParams(
            collective_id=0, has_side_effects=True, vmem_limit_bytes=60 * 1024 * 1024
        ),
    )(keep_tile.astype(jnp.int32), by_tile, integrals)


def solution(mesh):
    placed = (P("pair", None, "integral"), P(), P("pair", None, "integral"))
    return jax.shard_map(
        on_device, mesh=mesh, in_specs=placed, out_specs=P("pair", "integral"), check_vma=False
    )
```

```python
import functools
import itertools

import jax
import jax.numpy as jnp
from jax import lax
from jax.experimental import pallas as pl
from jax.experimental.pallas import tpu as pltpu
from jax.sharding import PartitionSpec as P

MESH = pl.DeviceIdType.MESH
CORES = 2
HALVES = 2
CUTS = 2
UNROLL = 4
MUL_LAG = 2
SUM_LAG = 3
WIDE = 512
AHEAD = ((-1, -1), (-1, -1), (-1, 1), (3, 4))
LAG = 2
LANES = 128
SUB = 8
LEVELS = 32766.0
TINY = 2e-34


def inner_of(count):
    return 2 ** ((count.bit_length() - 1) // 2)


def plan_of(count, cuts):
    steps = count * cuts
    if count & (count - 1):
        order = [[(k - z) % count for k in range(2 * z, 2 * z + count)] for z in range(count)]
    else:
        order = [[z ^ k ^ (k >> 1) for k in range(count)] for z in range(count)]
    late = {}
    for zc in range(count):
        for zs in (range(zc), range(count - 1, zc, -1)):
            before = None
            for z in zs:
                for r in range(cuts):
                    ready = order[z].index(zc) * cuts + r + SUM_LAG
                    late[z, zc, r] = ready if before is None else max(ready, late[before, zc, r] + LAG)
                before = z
    last = max(late.values())
    passes = [[[[] for _ in range(count)] for _ in range(cuts)] for _ in range(last + 1)]
    for (z, zc, r), at in late.items():
        if 0 < z < count - 1:
            passes[at][r][z].append(zc)
    return order, passes, max(last + 1, steps + SUM_LAG)


def release(k, r):
    return AHEAD[k][r] if k < len(AHEAD) else AHEAD[-1][r] + (k + 1 - len(AHEAD)) * CUTS


def ladder_kernel(
    dims, keep_ref, t2_ref, v_ref, out_ref,
    tiles, packed, result, amps, ints, part, y_out, y_scale, y_in, y_in_scale, z_out, z_scale, z_in, z_in_scale,
    v_sem, t_sem, own_sem, out_sem, a_send, a_recv, x_send, x_recv, c_send, c_recv, y_send, y_recv, z_send, z_recv,
):
    np_, ny, ni, slots, rows, cols = dims
    nz, nx = np_ // ny, ni // CORES
    piece = rows // CUTS
    kept = t2_ref.shape[0]
    qw = v_ref.shape[2]
    width = qw // HALVES
    p, i = lax.axis_index("pair"), lax.axis_index("integral")
    z, y = p // ny, p % ny
    x, c = i // CORES, i % CORES
    other = x * CORES + (1 - c)
    tables, passes, loops = plan_of(nz, CUTS)

    def pick(values):
        return sum(jnp.where(z == at, values[at], 0) for at in range(nz))

    order = [pick([tables[at][k] for at in range(nz)]) for k in range(nz)]

    load_t = pltpu.make_async_copy(t2_ref, tiles, t_sem)
    load_t.start()
    load_v = pltpu.make_async_copy(v_ref, ints, v_sem)

    barrier = pltpu.get_barrier_semaphore()
    for d in range(1, np_):
        pl.semaphore_signal(barrier, inc=1, device_id={"pair": (p + d) % np_}, device_id_type=MESH)
    for d in range(1, nx):
        pl.semaphore_signal(
            barrier, inc=1, device_id={"integral": ((x + d) % nx) * CORES + c}, device_id_type=MESH
        )
    pl.semaphore_signal(barrier, inc=1, device_id={"integral": other}, device_id_type=MESH)

    def places(owner):
        found = []
        for s in range(slots):
            tile = owner * slots + s
            at = jnp.int32(kept)
            for j in range(kept):
                at = jnp.where(keep_ref[j] == tile, j, at)
            found.append(at)
        return found

    def pack(owner, r, found):
        for s in range(slots):
            tile = tiles[jnp.minimum(found[s], kept - 1), r * piece : (r + 1) * piece, :]
            packed[owner, r, s] = jnp.where(found[s] < kept, tile, jnp.zeros_like(tile))

    def block(source, r, part_i):
        start = (((source // ny) * CUTS + r) * ny + source % ny) * piece
        return amps.at[part_i, :, pl.ds(pl.multiple_of(start, piece), piece), :]

    def a_copy(dest, source, r):
        return pltpu.make_async_remote_copy(
            src_ref=packed.at[dest, r], dst_ref=block(source, r, i),
            send_sem=a_send, recv_sem=a_recv.at[source, r],
            device_id={"pair": dest}, device_id_type=MESH,
        )

    def x_copy(source, r, dest_x, from_x):
        region = block(source, r, from_x * CORES + c)
        return pltpu.make_async_remote_copy(
            src_ref=region, dst_ref=region, send_sem=x_send, recv_sem=x_recv.at[from_x, source, r],
            device_id={"integral": dest_x * CORES + c}, device_id_type=MESH,
        )

    def c_copy(source, r, part_x, part_c):
        region = block(source, r, part_x * CORES + part_c)
        return pltpu.make_async_remote_copy(
            src_ref=region, dst_ref=region, send_sem=c_send, recv_sem=c_recv.at[part_x, source, r],
            device_id={"integral": other}, device_id_type=MESH,
        )

    def own_copy(r):
        return pltpu.make_async_copy(packed.at[p, r], block(p, r, i), own_sem.at[r])

    def y_copies(zc, r, d, h):
        pairs = ((y_out, y_in), (y_scale, y_in_scale))
        return [
            pltpu.make_async_remote_copy(
                src_ref=src.at[d - 1, zc, r, h], dst_ref=dst.at[d - 1, zc, r, h],
                send_sem=y_send.at[n], recv_sem=y_recv.at[n, d - 1, zc, r, h],
                device_id={"pair": z * ny + (y + d) % ny}, device_id_type=MESH,
            )
            for n, (src, dst) in enumerate(pairs)
        ]

    def z_copies(zc, slot, r, h):
        to = jnp.where(zc > z, p + ny, p + np_ - ny) % np_
        pairs = ((z_out, z_in), (z_scale, z_in_scale))
        return [
            pltpu.make_async_remote_copy(
                src_ref=src.at[zc, r, h], dst_ref=dst.at[slot, r, h],
                send_sem=z_send.at[n], recv_sem=z_recv.at[n, slot, r, h],
                device_id={"pair": to}, device_id_type=MESH,
            )
            for n, (src, dst) in enumerate(pairs)
        ]

    def z_slot(zc):
        return jnp.where(zc == z - 1, nz, zc)

    def lanes_of(g):
        return pl.ds(pl.multiple_of(g * LANES, LANES), LANES)

    def absorb(total, code, scale):
        step = scale[...]

        @pl.loop(0, width // LANES, unroll=UNROLL)
        def _(g):
            at = lanes_of(g)
            gain = code[:, at].astype(jnp.float32).reshape(piece // SUB, SUB, LANES) * step[None]
            total[:, at] += gain.reshape(piece, LANES)

    def encode(total, code, scale):
        def most(g, top):
            values = jnp.abs(total[:, lanes_of(g)]).reshape(piece // SUB, SUB, LANES)
            return jnp.maximum(top, jnp.max(values, axis=0))

        top = lax.fori_loop(0, width // LANES, most, jnp.full((SUB, LANES), TINY, jnp.float32), unroll=UNROLL)
        scale[...] = top * (1.0 / LEVELS)
        gain = LEVELS / top

        @pl.loop(0, width // LANES, unroll=UNROLL)
        def _(g):
            at = lanes_of(g)
            values = total[:, at].reshape(piece // SUB, SUB, LANES) * gain[None]
            code[:, at] = jnp.round(values).reshape(piece, LANES).astype(jnp.int32).astype(jnp.int16)

    load_t.wait()
    load_v.start()
    own_places = places(p)
    for r in range(CUTS):
        pack(p, r, own_places)
        own_copy(r).start()
    pl.semaphore_wait(barrier, np_ - 1 + nx - 1 + 1)

    def send_rows(k, r):
        plane = order[k]
        for dy in range(ny):
            dest = plane * ny + (y + dy) % ny
            if k or dy:
                if r == 0:
                    found[k, dy] = places(dest)
                    for each in range(CUTS):
                        pack(dest, each, found[k, dy])
                a_copy(dest, p, r).start()

    found = {}

    def sources(k):
        zc = order[k]
        for dy in range(ny):
            yield dy, zc * ny + (y + ny - dy) % ny

    def spread_one(source, r):
        for d in range(1, nx):
            x_copy(source, r, (x + d) % nx, x).start()
        c_copy(source, r, x, c).start()

    def spread(k, r):
        for dy, source in sources(k):
            if k or dy:
                a_copy(p, source, r).wait_recv()
                spread_one(source, r)

    def first():
        for r in range(CUTS):
            own_copy(r).wait()
            spread_one(p, r)
            for k in range(nz):
                if release(k, r) < 0:
                    send_rows(k, r)

    def forward(k, r):
        for dy, source in sources(k):
            for d in range(1, nx):
                from_x = (x + d) % nx
                x_copy(source, r, x, from_x).wait_recv()
                c_copy(source, r, from_x, c).start()

    def multiply(k, r):
        zc = order[k]
        for dy, source in sources(k):
            for xx in range(nx):
                c_copy(source, r, xx, 1 - c).wait_recv()
        if k == 0 and r == 0:
            load_v.wait()
        span = ny * piece
        left = pl.ds(pl.multiple_of((zc * CUTS + r) * span, span), span)
        wide = min(WIDE, width)
        for h in range(HALVES):
            @pl.loop(0, width // wide)
            def _(n):
                right = pl.ds(pl.multiple_of(h * width + n * wide, wide), wide)
                into = pl.ds(pl.multiple_of(n * wide, wide), wide)
                total = jnp.zeros((span, wide), jnp.float32)
                for s, at in itertools.product(range(slots), range(ni)):
                    inner = slice(at * cols, (at + 1) * cols)
                    total += jnp.dot(amps[at, s, left, :], ints[s, inner, right], preferred_element_type=jnp.float32)
                part[zc, r, h, :, :, into] = total.reshape(ny, piece, wide)

            for d in range(1, ny):
                encode(part.at[zc, r, h, (y + d) % ny], y_out.at[d - 1, zc, r, h], y_scale.at[d - 1, zc, r, h])
                for copy in y_copies(zc, r, d, h):
                    copy.start()

    def hand_on(zc, r, h):
        encode(part.at[zc, r, h, y], z_out.at[zc, r, h], z_scale.at[zc, r, h])
        for copy in z_copies(zc, z_slot(zc), r, h):
            copy.start()

    def take(slot, zc, r, h):
        for copy in z_copies(zc, slot, r, h):
            copy.wait_recv()
        absorb(part.at[zc, r, h, y], z_in.at[slot, r, h], z_in_scale.at[slot, r, h])

    def reduce_y(k, r):
        zc = order[k]
        for h in range(HALVES):
            for d in range(1, ny):
                for copy in y_copies(zc, r, d, h):
                    copy.wait_recv()
                absorb(part.at[zc, r, h, y], y_in.at[d - 1, zc, r, h], y_in_scale.at[d - 1, zc, r, h])
            if k > 0:
                @pl.when((z == 0) | (z == nz - 1))
                def _():
                    hand_on(zc, r, h)

    def pass_on(at):
        for r in range(CUTS if at < len(passes) else 0):
            now = passes[at][r]
            for n in range(max(len(some) for some in now)):
                to = [some[n] if n < len(some) else -1 for some in now]
                zc = pick([max(each, 0) for each in to])

                @pl.when(pick([int(each >= 0) for each in to]) > 0)
                def _():
                    for h in range(HALVES):
                        take(zc, zc, r, h)
                        hand_on(zc, r, h)

    steps = list(itertools.product(range(nz), range(CUTS)))
    first()
    last = len(steps) - 1
    early = nz > 2 and tables[0].index(1) * CUTS + CUTS - 1 + SUM_LAG <= last

    def take_early():
        for r, h in itertools.product(range(CUTS), range(HALVES)):
            pl.when(z == 1)(functools.partial(take, z, z, r, h))
            pl.when(z == nz - 2)(functools.partial(take, nz, z, r, h))

    for t in range(last):
        for ahead in steps:
            if release(*ahead) == t:
                send_rows(*ahead)
        spread(*steps[t])
        if t >= 1:
            forward(*steps[t - 1])
        if t >= MUL_LAG:
            multiply(*steps[t - MUL_LAG])
        if t >= SUM_LAG:
            reduce_y(*steps[t - SUM_LAG])
        if t < len(passes):
            pass_on(t)
    spread(*steps[last])
    forward(*steps[last - 1])
    multiply(*steps[last - 2])
    multiply(*steps[last - 1])
    reduce_y(*steps[last - 3])
    pass_on(last)
    if early:
        take_early()
    forward(*steps[last])
    reduce_y(*steps[last - 2])
    pass_on(last + 1)
    multiply(*steps[last])
    reduce_y(*steps[last - 1])
    pass_on(last + 2)
    reduce_y(*steps[last])
    for t in range(last + 3, len(passes)):
        pass_on(t)

    def sent(ref, sem):
        pltpu.make_async_copy(ref, ref, sem).wait()

    sent(packed.at[: np_ - 1], a_send)
    sent(amps.at[: nx - 1], x_send)
    sent(amps.at[:nx], c_send)
    sent(y_out, y_send.at[0])
    sent(y_scale, y_send.at[1])

    def out_copy(r):
        at = slice(r * piece, (r + 1) * piece)
        return pltpu.make_async_copy(result.at[at, :], out_ref.at[at, :], out_sem.at[r])

    for r, h in itertools.product(range(CUTS), range(HALVES)):
        @pl.when(z > int(early))
        def _():
            take(z, z, r, h)

        @pl.when(z < nz - 1 - int(early))
        def _():
            take(nz, z, r, h)

        result[r * piece : (r + 1) * piece, h * width : (h + 1) * width] = (0.5 * part[z, r, h, y]).astype(result.dtype)
        if h == HALVES - 1:
            out_copy(r).start()

    sent(z_out.at[: nz - 1], z_send.at[0])
    sent(z_scale.at[: nz - 1], z_send.at[1])
    for r in range(CUTS):
        out_copy(r).wait()


def on_device(t2_tiles, keep_tile, integrals):
    np_, ni = lax.axis_size("pair"), lax.axis_size("integral")
    rows, kept, cols = t2_tiles.shape
    slots, tt, qw = integrals.shape
    ny = inner_of(np_)
    nz, nx = np_ // ny, ni // CORES
    by_tile = jnp.swapaxes(t2_tiles, 0, 1)
    dma = pltpu.SemaphoreType.DMA
    piece, width = rows // CUTS, qw // HALVES
    dims = (np_, ny, ni, slots, rows, cols)
    y_lead, z_lead, in_lead = (ny - 1, nz, CUTS, HALVES), (nz, CUTS, HALVES), (nz + 1, CUTS, HALVES)
    return pl.pallas_call(
        functools.partial(ladder_kernel, dims),
        out_shape=jax.ShapeDtypeStruct((rows, qw), jnp.bfloat16),
        in_specs=[
            pl.BlockSpec(memory_space=pltpu.SMEM),
            pl.BlockSpec(memory_space=pl.ANY),
            pl.BlockSpec(memory_space=pl.ANY),
        ],
        out_specs=pl.BlockSpec(memory_space=pl.ANY),
        scratch_shapes=[
            pltpu.VMEM((kept, rows, cols), jnp.bfloat16),
            pltpu.VMEM((np_, CUTS, slots, piece, cols), jnp.bfloat16),
            pltpu.VMEM((rows, qw), jnp.bfloat16),
            pltpu.VMEM((ni, slots, np_ * rows, cols), jnp.bfloat16),
            pltpu.VMEM((slots, tt, qw), jnp.bfloat16),
            pltpu.VMEM((nz, CUTS, HALVES, ny, piece, width), jnp.float32),
            pltpu.VMEM((*y_lead, piece, width), jnp.int16),
            pltpu.VMEM((*y_lead, SUB, LANES), jnp.float32),
            pltpu.VMEM((*y_lead, piece, width), jnp.int16),
            pltpu.VMEM((*y_lead, SUB, LANES), jnp.float32),
            pltpu.VMEM((*z_lead, piece, width), jnp.int16),
            pltpu.VMEM((*z_lead, SUB, LANES), jnp.float32),
            pltpu.VMEM((*in_lead, piece, width), jnp.int16),
            pltpu.VMEM((*in_lead, SUB, LANES), jnp.float32),
            dma, dma, dma((CUTS,)), dma((CUTS,)),
            dma, dma((np_, CUTS)),
            dma, dma((nx, np_, CUTS)),
            dma, dma((nx, np_, CUTS)),
            dma((2,)), dma((2, *y_lead)),
            dma((2,)), dma((2, *in_lead)),
        ],
        compiler_params=pltpu.CompilerParams(
            collective_id=0, has_side_effects=True, vmem_limit_bytes=60 * 1024 * 1024
        ),
    )(keep_tile.astype(jnp.int32), by_tile, integrals)


def solution(mesh):
    placed = (P("pair", None, "integral"), P(), P("pair", None, "integral"))
    return jax.shard_map(
        on_device, mesh=mesh, in_specs=placed, out_specs=P("pair", "integral"), check_vma=False
    )
```

```python
import functools
import itertools

import jax
import jax.numpy as jnp
from jax import lax
from jax.experimental import pallas as pl
from jax.experimental.pallas import tpu as pltpu
from jax.sharding import PartitionSpec as P

MESH = pl.DeviceIdType.MESH
CORES = 2
HALVES = 2
CUTS = 2
UNROLL = 4
MUL_LAG = 2
SUM_LAG = 3
WIDE = 512
AHEAD = ((-1, -1), (-1, -1), (-1, 1), (3, 4))
LAG = 2
LANES = 128
SUB = 8
LEVELS = 32766.0
TINY = 2e-34


def inner_of(count):
    return 2 ** ((count.bit_length() - 1) // 2)


def plan_of(count, cuts):
    steps = count * cuts
    if count & (count - 1):
        order = [[(k - z) % count for k in range(2 * z, 2 * z + count)] for z in range(count)]
    else:
        order = [[z ^ k ^ (k >> 1) for k in range(count)] for z in range(count)]
    late = {}
    for zc in range(count):
        for zs in (range(zc), range(count - 1, zc, -1)):
            before = None
            for z in zs:
                for r in range(cuts):
                    ready = order[z].index(zc) * cuts + r + SUM_LAG
                    late[z, zc, r] = ready if before is None else max(ready, late[before, zc, r] + LAG)
                before = z
    last = max(late.values())
    passes = [[[[] for _ in range(count)] for _ in range(cuts)] for _ in range(last + 1)]
    for (z, zc, r), at in late.items():
        if 0 < z < count - 1:
            passes[at][r][z].append(zc)
    return order, passes, max(last + 1, steps + SUM_LAG)


def release(k, r):
    return AHEAD[k][r] if k < len(AHEAD) else AHEAD[-1][r] + (k + 1 - len(AHEAD)) * CUTS


def ladder_kernel(
    dims, keep_ref, t2_ref, v_ref, out_ref,
    tiles, packed, result, amps, ints, part, y_out, y_scale, y_in, y_in_scale, z_out, z_scale, z_in, z_in_scale,
    v_sem, t_sem, own_sem, out_sem, a_send, a_recv, x_send, x_recv, c_send, c_recv, y_send, y_recv, z_send, z_recv,
):
    np_, ny, ni, slots, rows, cols = dims
    nz, nx = np_ // ny, ni // CORES
    piece = rows // CUTS
    kept = t2_ref.shape[0]
    qw = v_ref.shape[2]
    width = qw // HALVES
    p, i = lax.axis_index("pair"), lax.axis_index("integral")
    z, y = p // ny, p % ny
    x, c = i // CORES, i % CORES
    other = x * CORES + (1 - c)
    tables, passes, loops = plan_of(nz, CUTS)

    def pick(values):
        return sum(jnp.where(z == at, values[at], 0) for at in range(nz))

    order = [pick([tables[at][k] for at in range(nz)]) for k in range(nz)]

    load_t = pltpu.make_async_copy(t2_ref, tiles, t_sem)
    load_t.start()
    load_v = pltpu.make_async_copy(v_ref, ints, v_sem)

    barrier = pltpu.get_barrier_semaphore()
    for d in range(1, np_):
        pl.semaphore_signal(barrier, inc=1, device_id={"pair": (p + d) % np_}, device_id_type=MESH)
    for d in range(1, nx):
        pl.semaphore_signal(
            barrier, inc=1, device_id={"integral": ((x + d) % nx) * CORES + c}, device_id_type=MESH
        )
    pl.semaphore_signal(barrier, inc=1, device_id={"integral": other}, device_id_type=MESH)

    def places(owner):
        found = []
        for s in range(slots):
            tile = owner * slots + s
            at = jnp.int32(kept)
            for j in range(kept):
                at = jnp.where(keep_ref[j] == tile, j, at)
            found.append(at)
        return found

    def pack(owner, r, found):
        for s in range(slots):
            tile = tiles[jnp.minimum(found[s], kept - 1), r * piece : (r + 1) * piece, :]
            packed[owner, r, s] = jnp.where(found[s] < kept, tile, jnp.zeros_like(tile))

    def block(source, r, part_i):
        start = (((source // ny) * CUTS + r) * ny + source % ny) * piece
        return amps.at[part_i, :, pl.ds(pl.multiple_of(start, piece), piece), :]

    def a_copy(dest, source, r):
        return pltpu.make_async_remote_copy(
            src_ref=packed.at[dest, r], dst_ref=block(source, r, i),
            send_sem=a_send, recv_sem=a_recv.at[source, r],
            device_id={"pair": dest}, device_id_type=MESH,
        )

    def x_copy(source, r, dest_x, from_x):
        region = block(source, r, from_x * CORES + c)
        away = (dest_x - from_x + nx) % nx - 1
        return pltpu.make_async_remote_copy(
            src_ref=region, dst_ref=region, send_sem=x_send, recv_sem=x_recv.at[away, source, r],
            device_id={"integral": dest_x * CORES + c}, device_id_type=MESH,
        )

    def c_copy(source, r, part_x, part_c):
        region = block(source, r, part_x * CORES + part_c)
        return pltpu.make_async_remote_copy(
            src_ref=region, dst_ref=region, send_sem=c_send, recv_sem=c_recv.at[part_x, source, r],
            device_id={"integral": other}, device_id_type=MESH,
        )

    def own_copy(r):
        return pltpu.make_async_copy(packed.at[p, r], block(p, r, i), own_sem.at[r])

    def y_copies(zc, r, d, h):
        pairs = ((y_out, y_in), (y_scale, y_in_scale))
        return [
            pltpu.make_async_remote_copy(
                src_ref=src.at[d - 1, zc, r, h], dst_ref=dst.at[d - 1, zc, r, h],
                send_sem=y_send.at[n], recv_sem=y_recv.at[n, d - 1, zc, r, h],
                device_id={"pair": z * ny + (y + d) % ny}, device_id_type=MESH,
            )
            for n, (src, dst) in enumerate(pairs)
        ]

    def z_copies(zc, slot, r, h):
        to = jnp.where(zc > z, p + ny, p + np_ - ny) % np_
        pairs = ((z_out, z_in), (z_scale, z_in_scale))
        return [
            pltpu.make_async_remote_copy(
                src_ref=src.at[zc, r, h], dst_ref=dst.at[slot, r, h],
                send_sem=z_send.at[n], recv_sem=z_recv.at[n, slot, r, h],
                device_id={"pair": to}, device_id_type=MESH,
            )
            for n, (src, dst) in enumerate(pairs)
        ]

    def z_slot(zc):
        return jnp.where(zc == z - 1, nz, zc)

    def lanes_of(g):
        return pl.ds(pl.multiple_of(g * LANES, LANES), LANES)

    def absorb(total, code, scale):
        step = scale[...]

        @pl.loop(0, width // LANES, unroll=UNROLL)
        def _(g):
            at = lanes_of(g)
            gain = code[:, at].astype(jnp.float32).reshape(piece // SUB, SUB, LANES) * step[None]
            total[:, at] += gain.reshape(piece, LANES)

    def encode(total, code, scale):
        def most(g, top):
            values = jnp.abs(total[:, lanes_of(g)]).reshape(piece // SUB, SUB, LANES)
            return jnp.maximum(top, jnp.max(values, axis=0))

        top = lax.fori_loop(0, width // LANES, most, jnp.full((SUB, LANES), TINY, jnp.float32), unroll=UNROLL)
        scale[...] = top * (1.0 / LEVELS)
        gain = LEVELS / top

        @pl.loop(0, width // LANES, unroll=UNROLL)
        def _(g):
            at = lanes_of(g)
            values = total[:, at].reshape(piece // SUB, SUB, LANES) * gain[None]
            code[:, at] = jnp.round(values).reshape(piece, LANES).astype(jnp.int32).astype(jnp.int16)

    load_t.wait()
    load_v.start()
    own_places = places(p)
    for r in range(CUTS):
        pack(p, r, own_places)
        own_copy(r).start()
    pl.semaphore_wait(barrier, np_ - 1 + nx - 1 + 1)

    def send_rows(k, r):
        plane = order[k]
        for dy in range(ny):
            dest = plane * ny + (y + dy) % ny
            if k or dy:
                if r == 0:
                    found[k, dy] = places(dest)
                    for each in range(CUTS):
                        pack(dest, each, found[k, dy])
                a_copy(dest, p, r).start()

    found = {}

    def sources(k):
        zc = order[k]
        for dy in range(ny):
            yield dy, zc * ny + (y + ny - dy) % ny

    def spread_one(source, r):
        for d in range(1, nx):
            x_copy(source, r, (x + d) % nx, x).start()
        c_copy(source, r, x, c).start()

    def spread(k, r):
        for dy, source in sources(k):
            if k or dy:
                a_copy(p, source, r).wait_recv()
                spread_one(source, r)

    def first():
        for r in range(CUTS):
            own_copy(r).wait()
            spread_one(p, r)
            for k in range(nz):
                if release(k, r) < 0:
                    send_rows(k, r)

    def forward(k, r):
        for dy, source in sources(k):
            for d in range(1, nx):
                from_x = (x + d) % nx
                x_copy(source, r, x, from_x).wait_recv()
                c_copy(source, r, from_x, c).start()

    def multiply(k, r):
        zc = order[k]
        for dy, source in sources(k):
            for xx in range(nx):
                c_copy(source, r, xx, 1 - c).wait_recv()
        if k == 0 and r == 0:
            load_v.wait()
        span = ny * piece
        left = pl.ds(pl.multiple_of((zc * CUTS + r) * span, span), span)
        wide = min(WIDE, width)
        for h in range(HALVES):
            @pl.loop(0, width // wide)
            def _(n):
                right = pl.ds(pl.multiple_of(h * width + n * wide, wide), wide)
                into = pl.ds(pl.multiple_of(n * wide, wide), wide)
                total = jnp.zeros((span, wide), jnp.float32)
                for s, at in itertools.product(range(slots), range(ni)):
                    inner = slice(at * cols, (at + 1) * cols)
                    total += jnp.dot(amps[at, s, left, :], ints[s, inner, right], preferred_element_type=jnp.float32)
                part[zc, r, h, :, :, into] = total.reshape(ny, piece, wide)

            for d in range(1, ny):
                encode(part.at[zc, r, h, (y + d) % ny], y_out.at[d - 1, zc, r, h], y_scale.at[d - 1, zc, r, h])
                for copy in y_copies(zc, r, d, h):
                    copy.start()

    def hand_on(zc, r, h):
        encode(part.at[zc, r, h, y], z_out.at[zc, r, h], z_scale.at[zc, r, h])
        for copy in z_copies(zc, z_slot(zc), r, h):
            copy.start()

    def take(slot, zc, r, h):
        for copy in z_copies(zc, slot, r, h):
            copy.wait_recv()
        absorb(part.at[zc, r, h, y], z_in.at[slot, r, h], z_in_scale.at[slot, r, h])

    def reduce_y(k, r):
        zc = order[k]
        for h in range(HALVES):
            for d in range(1, ny):
                for copy in y_copies(zc, r, d, h):
                    copy.wait_recv()
                absorb(part.at[zc, r, h, y], y_in.at[d - 1, zc, r, h], y_in_scale.at[d - 1, zc, r, h])
            if k > 0:
                @pl.when((z == 0) | (z == nz - 1))
                def _():
                    hand_on(zc, r, h)

    def pass_on(at):
        for r in range(CUTS if at < len(passes) else 0):
            now = passes[at][r]
            for n in range(max(len(some) for some in now)):
                to = [some[n] if n < len(some) else -1 for some in now]
                zc = pick([max(each, 0) for each in to])

                @pl.when(pick([int(each >= 0) for each in to]) > 0)
                def _():
                    for h in range(HALVES):
                        take(zc, zc, r, h)
                        hand_on(zc, r, h)

    steps = list(itertools.product(range(nz), range(CUTS)))
    first()
    last = len(steps) - 1
    early = nz > 2 and tables[0].index(1) * CUTS + CUTS - 1 + SUM_LAG <= last

    def take_early():
        for r, h in itertools.product(range(CUTS), range(HALVES)):
            pl.when(z == 1)(functools.partial(take, z, z, r, h))
            pl.when(z == nz - 2)(functools.partial(take, nz, z, r, h))

    for t in range(last):
        for ahead in steps:
            if release(*ahead) == t:
                send_rows(*ahead)
        spread(*steps[t])
        if t >= 1:
            forward(*steps[t - 1])
        if t >= MUL_LAG:
            multiply(*steps[t - MUL_LAG])
        if t >= SUM_LAG:
            reduce_y(*steps[t - SUM_LAG])
        if t < len(passes):
            pass_on(t)
    spread(*steps[last])
    forward(*steps[last - 1])
    multiply(*steps[last - 2])
    multiply(*steps[last - 1])
    reduce_y(*steps[last - 3])
    pass_on(last)
    if early:
        take_early()
    forward(*steps[last])
    reduce_y(*steps[last - 2])
    pass_on(last + 1)
    multiply(*steps[last])
    reduce_y(*steps[last - 1])
    pass_on(last + 2)
    reduce_y(*steps[last])
    for t in range(last + 3, len(passes)):
        pass_on(t)

    def sent(ref, sem):
        pltpu.make_async_copy(ref, ref, sem).wait()

    sent(packed.at[: np_ - 1], a_send)
    sent(amps.at[: nx - 1], x_send)
    sent(amps.at[:nx], c_send)
    sent(y_out, y_send.at[0])
    sent(y_scale, y_send.at[1])

    def out_copy(r):
        at = slice(r * piece, (r + 1) * piece)
        return pltpu.make_async_copy(result.at[at, :], out_ref.at[at, :], out_sem.at[r])

    for r, h in itertools.product(range(CUTS), range(HALVES)):
        @pl.when(z > int(early))
        def _():
            take(z, z, r, h)

        @pl.when(z < nz - 1 - int(early))
        def _():
            take(nz, z, r, h)

        result[r * piece : (r + 1) * piece, h * width : (h + 1) * width] = (0.5 * part[z, r, h, y]).astype(result.dtype)
        if h == HALVES - 1:
            out_copy(r).start()

    sent(z_out.at[: nz - 1], z_send.at[0])
    sent(z_scale.at[: nz - 1], z_send.at[1])
    for r in range(CUTS):
        out_copy(r).wait()


def on_device(t2_tiles, keep_tile, integrals):
    np_, ni = lax.axis_size("pair"), lax.axis_size("integral")
    rows, kept, cols = t2_tiles.shape
    slots, tt, qw = integrals.shape
    ny = inner_of(np_)
    nz, nx = np_ // ny, ni // CORES
    by_tile = jnp.swapaxes(t2_tiles, 0, 1)
    dma = pltpu.SemaphoreType.DMA
    piece, width = rows // CUTS, qw // HALVES
    dims = (np_, ny, ni, slots, rows, cols)
    y_lead, z_lead, in_lead = (ny - 1, nz, CUTS, HALVES), (nz, CUTS, HALVES), (nz + 1, CUTS, HALVES)
    return pl.pallas_call(
        functools.partial(ladder_kernel, dims),
        out_shape=jax.ShapeDtypeStruct((rows, qw), jnp.bfloat16),
        in_specs=[
            pl.BlockSpec(memory_space=pltpu.SMEM),
            pl.BlockSpec(memory_space=pl.ANY),
            pl.BlockSpec(memory_space=pl.ANY),
        ],
        out_specs=pl.BlockSpec(memory_space=pl.ANY),
        scratch_shapes=[
            pltpu.VMEM((kept, rows, cols), jnp.bfloat16),
            pltpu.VMEM((np_, CUTS, slots, piece, cols), jnp.bfloat16),
            pltpu.VMEM((rows, qw), jnp.bfloat16),
            pltpu.VMEM((ni, slots, np_ * rows, cols), jnp.bfloat16),
            pltpu.VMEM((slots, tt, qw), jnp.bfloat16),
            pltpu.VMEM((nz, CUTS, HALVES, ny, piece, width), jnp.float32),
            pltpu.VMEM((*y_lead, piece, width), jnp.int16),
            pltpu.VMEM((*y_lead, SUB, LANES), jnp.float32),
            pltpu.VMEM((*y_lead, piece, width), jnp.int16),
            pltpu.VMEM((*y_lead, SUB, LANES), jnp.float32),
            pltpu.VMEM((*z_lead, piece, width), jnp.int16),
            pltpu.VMEM((*z_lead, SUB, LANES), jnp.float32),
            pltpu.VMEM((*in_lead, piece, width), jnp.int16),
            pltpu.VMEM((*in_lead, SUB, LANES), jnp.float32),
            dma, dma, dma((CUTS,)), dma((CUTS,)),
            dma, dma((np_, CUTS)),
            dma, dma((nx - 1, np_, CUTS)),
            dma, dma((nx, np_, CUTS)),
            dma((2,)), dma((2, *y_lead)),
            dma((2,)), dma((2, *in_lead)),
        ],
        compiler_params=pltpu.CompilerParams(
            collective_id=0, has_side_effects=True, vmem_limit_bytes=60 * 1024 * 1024
        ),
    )(keep_tile.astype(jnp.int32), by_tile, integrals)


def solution(mesh):
    placed = (P("pair", None, "integral"), P(), P("pair", None, "integral"))
    return jax.shard_map(
        on_device, mesh=mesh, in_specs=placed, out_specs=P("pair", "integral"), check_vma=False
    )
```
